32 devices in a mesh: groups: 2 (over x), frame: 16 (over z, y, core).
Axes of the slice: x: 2, y: 2, z: 4, core: 2. Of those that a mesh axis runs over, the one named last changes fastest.
Arguments:
- queries: bfloat16 [16384, 2560], P(('groups', 'frame')), parts along dimension 0, may hold values from -48 to 48, as said below
- keys_values: bfloat16 [16384, 2, 2560], P(('groups', 'frame')), parts along dimension 0, may hold values from -6 to 6, as said below
- offsets: int32 [128, 3], P(('groups', 'frame')), parts along dimension 0, may hold values from -2 to 2, as said below
- ref_owner: int32 [8], P('groups'), parts along dimension 0, may hold values from 0 to 15
- ref_slot: int32 [8], P('groups'), parts along dimension 0, may hold values from 0 to 2
Outputs:
- attended: bfloat16 [16384, 2560], P(('groups', 'frame')), parts along dimension 0
The draws below stay inside these ranges and needn't reach their ends.
There are 2 independent parts, one for each index of `groups`. The reference program is written for one: setup_inputs(seed, part) draws one part's arguments, and reference() takes and returns one part's arrays. A program takes and returns all parts, laid end to end along the dimension named above; each array names one. Nothing has to cross between parts.
Inputs may be any that keep to these rules, and one draw needn't show every extreme that they name: `queries`: custom draw; aside from the table's range nothing further. `keys_values`: custom draw. `offsets`: each row holds 3 different nonzero numbers.
All inputs are finite; a program needn't handle non-finite values.
Results may differ from the reference program's by a relative error of at most 0.0047.
Values may be sent and summed in bfloat16 or wider, within the bound.
No kernel may reach another device: no remote copies, remote signals or barrier semaphores. Data moves between devices by JAX's collectives and lax.ppermute only.
A program may use at most 128 MiB of HBM per device.

```python
import math
import jax
import jax.numpy as jnp
from jax import lax

H = 20
DH = 128
BLK = 128
WIN = 3
REACH = 2
NREF = 4
REFLEN = 256
TOK_DEV = 512
TOKENS = 8192
NBLK = 64
N_FRAME = 16


def make_pair(key):
    full_shape = (TOKENS, H * DH)
    query_key = jax.random.fold_in(key, 301)
    key_key = jax.random.fold_in(key, 302)
    value_key = jax.random.fold_in(key, 303)
    values = jax.random.truncated_normal(value_key, -5.0, 5.0, full_shape, jnp.float32)
    queries = jax.random.truncated_normal(query_key, -5.0, 5.0, full_shape, jnp.float32)
    key_rows = jax.random.truncated_normal(key_key, -5.0, 5.0, full_shape, jnp.float32)
    return (queries, jnp.stack([key_rows, values], axis=1))


def draw_queries(key, part):
    return make_pair(key)[0].astype(jnp.bfloat16)


def draw_keys_values(key, part):
    return make_pair(key)[1].astype(jnp.bfloat16)


def draw_offsets(key, part):
    scores = jax.random.randint(key, (NBLK, 2 * REACH), 0, 1000) * (2 * REACH) + jnp.arange(2 * REACH)
    order = jnp.argsort(scores, axis=1)[:, :WIN]
    candidates = jnp.arange(2 * REACH) - REACH
    candidates = candidates + (candidates >= 0).astype(jnp.int32)
    return candidates[order].astype(jnp.int32)


def set_ends(values, stream_key, smallest, top_value):
    shape = values.shape
    index_at = [jax.random.randint(jax.random.fold_in(stream_key, axis), (), 0, shape[axis]) for axis in range(len(shape))]
    values = values.at[tuple(index_at)].set(smallest)
    longest = shape.index(max(shape))
    index_at[longest] = (index_at[longest] + 1) % shape[longest]
    return values.at[tuple(index_at)].set(top_value)


def setup_inputs(seed: int = 0, part: int = 0) -> dict:
    splits = jax.random.split(jax.random.key(seed), 6)
    part_splits = jax.random.split(jax.random.fold_in(splits[5], part), 6)
    return {
        "queries": draw_queries(jax.random.fold_in(jax.random.fold_in(splits[5], part), 71), part),
        "keys_values": draw_keys_values(jax.random.fold_in(jax.random.fold_in(splits[5], part), 71), part),
        "offsets": draw_offsets(jax.random.fold_in(jax.random.fold_in(splits[5], part), 71), part),
        "ref_owner": set_ends(jax.random.randint(part_splits[3], (NREF,), 0, N_FRAME), jax.random.fold_in(part_splits[3], 1), 0, N_FRAME - 1).astype(jnp.int32),
        "ref_slot": set_ends(jax.random.randint(part_splits[4], (NREF,), 0, (TOK_DEV - REFLEN) // BLK + 1), jax.random.fold_in(part_splits[4], 1), 0, ((TOK_DEV - REFLEN) // BLK + 1) - 1).astype(jnp.int32),
    }


def reference(queries, keys_values, offsets, ref_owner, ref_slot):
    tok_rows = queries.shape[0]
    columns = queries.shape[1]
    head_count = columns // DH
    block_count = tok_rows // BLK
    score_scale = 1.0 / math.sqrt(DH)
    starts = (ref_owner * TOK_DEV + ref_slot * BLK).astype(jnp.int32)
    ref_pairs = jnp.concatenate([lax.dynamic_slice_in_dim(keys_values, starts[slot_id], REFLEN, 0) for slot_id in range(NREF)], 0)
    ref_keys = ref_pairs[:, 0].reshape(NREF * REFLEN, head_count, DH).astype(jnp.float32)
    ref_values = ref_pairs[:, 1].reshape(NREF * REFLEN, head_count, DH).astype(jnp.float32)
    margin = REACH * BLK
    padded = jnp.pad(keys_values, ((margin, margin), (0, 0), (0, 0)))

    def one_block(block_id):
        query_rows = lax.dynamic_slice_in_dim(queries, block_id * BLK, BLK, 0).reshape(BLK, head_count, DH).astype(jnp.float32)
        block_offsets = jnp.concatenate([jnp.zeros((1,), jnp.int32), offsets[block_id].astype(jnp.int32)])
        listed = jnp.stack([lax.dynamic_slice_in_dim(padded, ((block_id + block_offsets[slot_id]) * BLK + margin).astype(jnp.int32), BLK, 0) for slot_id in range(1 + WIN)])
        target = block_id + block_offsets
        usable = (target >= 0) & (target < block_count)
        key_mask = jnp.repeat(usable, BLK)
        win_keys = listed[:, :, 0].reshape((1 + WIN) * BLK, head_count, DH).astype(jnp.float32)
        win_values = listed[:, :, 1].reshape((1 + WIN) * BLK, head_count, DH).astype(jnp.float32)
        window_scores = jnp.einsum('qhd,khd->hqk', query_rows, win_keys) * score_scale
        window_scores = jnp.where(key_mask[None, None, :], window_scores, -jnp.inf)
        ref_scores = jnp.einsum('qhd,khd->hqk', query_rows, ref_keys) * score_scale
        row_max = jnp.maximum(lax.optimization_barrier(jnp.max(window_scores, -1)), lax.optimization_barrier(jnp.max(ref_scores, -1)))
        window_probs = jnp.exp(window_scores - row_max[..., None])
        ref_probs = jnp.exp(ref_scores - row_max[..., None])
        totals = lax.optimization_barrier(jnp.sum(window_probs, -1)) + lax.optimization_barrier(jnp.sum(ref_probs, -1))
        window_weights = lax.optimization_barrier(window_probs.astype(jnp.bfloat16)).astype(jnp.float32)
        ref_weights = lax.optimization_barrier(ref_probs.astype(jnp.bfloat16)).astype(jnp.float32)
        weighted = jnp.einsum('hqk,khd->qhd', window_weights, win_values) + jnp.einsum('hqk,khd->qhd', ref_weights, ref_values)
        result = weighted / jnp.transpose(totals)[..., None]
        return result.astype(jnp.bfloat16).reshape(BLK, columns)
    stacked = lax.map(one_block, jnp.arange(block_count, dtype=jnp.int32))
    return stacked.reshape(tok_rows, columns)
```

```python
import functools
import math

import jax
import jax.numpy as jnp
from jax import lax
from jax.experimental import pallas as pl
from jax.experimental.pallas import tpu as pltpu
from jax.sharding import PartitionSpec as P

DH = 128
BLK = 128
WIN = 3
REACH = 2
NREF = 4
REFLEN = 256
SCALE = math.log2(math.e) / math.sqrt(DH)
MASKED = -1e30


def cost(flops, moved, exps):
    return pl.CostEstimate(flops=flops, bytes_accessed=moved, transcendentals=exps)


def split_kernel(core_ref, kv_ref, mine_ref, theirs_ref):
    half = mine_ref.shape[2]
    core = core_ref[0]
    for out_ref, side in ((mine_ref, core), (theirs_ref, 1 - core)):
        start = pl.multiple_of(side * half, DH)
        for which in range(2):
            out_ref[which] = kv_ref[:, which, pl.ds(start, half)]


def split_columns(core, keys_values):
    rows, _, columns = keys_values.shape
    half = columns // 2
    step = 64
    out_spec = pl.BlockSpec((2, step, half), lambda i, c: (0, i, 0))
    return pl.pallas_call(
        split_kernel,
        out_shape=[jax.ShapeDtypeStruct((2, rows, half), keys_values.dtype)] * 2,
        grid_spec=pltpu.PrefetchScalarGridSpec(
            num_scalar_prefetch=1,
            grid=(rows // step,),
            in_specs=[pl.BlockSpec((step, 2, columns), lambda i, c: (i, 0, 0))],
            out_specs=[out_spec] * 2,
        ),
        cost_estimate=cost(0, 4 * rows * columns * 2, 0),
        name="split_columns",
    )(core, keys_values)


def attend(query, keys, values, biases, state):
    scores = []
    for key, bias in zip(keys, biases):
        s = lax.dot_general(
            key, query, (((1,), (1,)), ((), ())), preferred_element_type=jnp.float32
        )
        scores.append(s if bias is None else s + bias)
    top = functools.reduce(jnp.maximum, [jnp.max(s, 0, keepdims=True) for s in scores])
    if state is not None:
        old_top, old_total, old_sum = state
        top = jnp.maximum(top, old_top)
    total = None
    summed = None
    for s, value in zip(scores, values):
        probs = jnp.exp2((s - top) * SCALE)
        part = jnp.sum(probs, 0, keepdims=True)
        total = part if total is None else total + part
        part = lax.dot_general(
            value,
            probs.astype(jnp.bfloat16),
            (((0,), (0,)), ((), ())),
            preferred_element_type=jnp.float32,
        )
        summed = part if summed is None else summed + part
    if state is not None:
        fade = jnp.exp2((old_top - top) * SCALE)
        total = total + fade * old_total
        summed = summed + fade * old_sum
    return top, total, summed


def window_kernel(table, qm_ref, qo_ref, mine, other, left, right, sum_ref, top_ref, total_ref, ext):
    rows = mine.shape[1]
    margin = left.shape[1]
    core = table[0]
    blocks = rows // BLK
    for which in range(2):
        ext[which, 0:margin] = left[which]
        ext[which, pl.ds(pl.multiple_of(margin + core * rows, BLK), rows)] = mine[which]
        ext[which, pl.ds(pl.multiple_of(margin + (1 - core) * rows, BLK), rows)] = other[which]
        ext[which, margin + 2 * rows : 2 * margin + 2 * rows] = right[which]
    count = 2 * blocks * (1 + WIN)
    for block in range(2 * blocks):
        q_ref = qm_ref if block < blocks else qo_ref
        at = (block % blocks) * BLK
        query = q_ref[at : at + BLK, :]
        keys, values, biases = [], [], []
        for listed in range(1 + WIN):
            entry = 1 + block * (1 + WIN) + listed
            start = pl.multiple_of(table[entry] * BLK, BLK)
            keys.append(ext[0, pl.ds(start, BLK), :])
            values.append(ext[1, pl.ds(start, BLK), :])
            usable = table[count + entry]
            biases.append(None if listed == 0 else jnp.where(usable == 1, 0.0, MASKED))
        top, total, summed = attend(query, keys, values, biases, None)
        lanes = slice(block * BLK, (block + 1) * BLK)
        sum_ref[:, lanes] = summed
        top_ref[0, :, lanes] = top
        total_ref[0, :, lanes] = total


def window_part(table, queries, q_other, mine, other, left, right):
    rows, half = q_other.shape
    heads = half // DH
    margin = left.shape[1]
    lanes = 2 * rows
    head = lambda h, t: (0, h)
    head3 = lambda h, t: (0, 0, h)
    state = lambda h, t: (h, 0, 0)
    keys = 2 * rows * (1 + WIN) * BLK
    return pl.pallas_call(
        window_kernel,
        out_shape=[
            jax.ShapeDtypeStruct((half, lanes), jnp.float32),
            jax.ShapeDtypeStruct((heads, 1, lanes), jnp.float32),
            jax.ShapeDtypeStruct((heads, 1, lanes), jnp.float32),
        ],
        grid_spec=pltpu.PrefetchScalarGridSpec(
            num_scalar_prefetch=1,
            grid=(heads,),
            in_specs=[
                pl.BlockSpec((rows, DH), lambda h, t: (0, t[0] * heads + h)),
                pl.BlockSpec((rows, DH), head),
                pl.BlockSpec((2, rows, DH), head3),
                pl.BlockSpec((2, rows, DH), head3),
                pl.BlockSpec((2, margin, DH), head3),
                pl.BlockSpec((2, margin, DH), head3),
            ],
            out_specs=[
                pl.BlockSpec((DH, lanes), lambda h, t: (h, 0)),
                pl.BlockSpec((1, 1, lanes), state),
                pl.BlockSpec((1, 1, lanes), state),
            ],
            scratch_shapes=[pltpu.VMEM((2, 2 * rows + 2 * margin, DH), mine.dtype)],
        ),
        cost_estimate=cost(
            4 * keys * DH * heads, half * (lanes * 6 + 8 * (rows + margin)), keys * heads
        ),
        name="window_part",
    )(table, queries, q_other, mine, other, left, right)


def ref_kernel(count, chunk, core_ref, qm_ref, qo_ref, *refs):
    pieces = refs[:count]
    sum_in, top_in, total_in, sum_ref, top_ref, total_ref = refs[count:]
    rows = qm_ref.shape[0]
    keys = [piece[0] for piece in pieces]
    values = [piece[1] for piece in pieces]
    for part in range(2 * rows // chunk):
        lanes = slice(part * chunk, (part + 1) * chunk)
        q_ref = qm_ref if part * chunk < rows else qo_ref
        at = (part * chunk) % rows
        state = (top_in[0, :, lanes], total_in[0, :, lanes], sum_in[:, lanes])
        top, total, summed = attend(
            q_ref[at : at + chunk, :], keys, values, [None] * count, state
        )
        sum_ref[:, lanes] = summed
        top_ref[0, :, lanes] = top
        total_ref[0, :, lanes] = total


def ref_part(core, queries, q_other, pieces, state):
    rows, half = q_other.shape
    heads = half // DH
    lanes = 2 * rows
    head3 = lambda h, c: (0, 0, h)
    at_head = lambda h, c: (h, 0, 0)
    state_specs = [
        pl.BlockSpec((DH, lanes), lambda h, c: (h, 0)),
        pl.BlockSpec((1, 1, lanes), at_head),
        pl.BlockSpec((1, 1, lanes), at_head),
    ]
    listed = sum(piece.shape[1] for piece in pieces)
    count = len(pieces)
    return pl.pallas_call(
        functools.partial(ref_kernel, count, 2 * BLK),
        out_shape=[jax.ShapeDtypeStruct(s.shape, s.dtype) for s in state],
        grid_spec=pltpu.PrefetchScalarGridSpec(
            num_scalar_prefetch=1,
            grid=(heads,),
            in_specs=[
                pl.BlockSpec((rows, DH), lambda h, c: (0, c[0] * heads + h)),
                pl.BlockSpec((rows, DH), lambda h, c: (0, h)),
            ]
            + [pl.BlockSpec((2, piece.shape[1], DH), head3) for piece in pieces]
            + state_specs,
            out_specs=state_specs,
        ),
        input_output_aliases={3 + count + i: i for i in range(3)},
        cost_estimate=cost(
            4 * lanes * listed * half, half * (lanes * 10 + 4 * listed), lanes * listed * heads
        ),
        name="ref_part",
    )(core, queries, q_other, *pieces, *state)


def last_kernel(count, chunk, core_ref, q_ref, *refs):
    pieces = refs[:count]
    sum_in, top_in, total_in, out_ref = refs[count:]
    keys = [piece[0] for piece in pieces]
    values = [piece[1] for piece in pieces]
    for part in range(q_ref.shape[0] // chunk):
        lanes = slice(part * chunk, (part + 1) * chunk)
        state = (top_in[0, :, lanes], total_in[0, :, lanes], sum_in[:, lanes])
        _, total, summed = attend(q_ref[lanes, :], keys, values, [None] * count, state)
        result = summed * (1.0 / total)
        out_ref[lanes, :] = jnp.transpose(result).astype(out_ref.dtype)


def last_part(core, query, own, pieces, state):
    rows = query.shape[0]
    half = state[0].shape[0]
    heads = half // DH
    head3 = lambda h, c: (0, 0, h)
    side = 0 if own else 1
    at_head = lambda h, c: (h, 0, side)
    column = (lambda h, c: (0, c[0] * heads + h)) if own else (lambda h, c: (0, h))
    listed = sum(piece.shape[1] for piece in pieces)
    count = len(pieces)
    return pl.pallas_call(
        functools.partial(last_kernel, count, 2 * BLK),
        out_shape=jax.ShapeDtypeStruct(query.shape, query.dtype),
        grid_spec=pltpu.PrefetchScalarGridSpec(
            num_scalar_prefetch=1,
            grid=(heads,),
            in_specs=[pl.BlockSpec((rows, DH), column)]
            + [pl.BlockSpec((2, piece.shape[1], DH), head3) for piece in pieces]
            + [
                pl.BlockSpec((DH, rows), lambda h, c: (h, side)),
                pl.BlockSpec((1, 1, rows), at_head),
                pl.BlockSpec((1, 1, rows), at_head),
            ],
            out_specs=pl.BlockSpec((rows, DH), column),
        ),
        cost_estimate=cost(
            4 * rows * listed * half, half * (rows * 8 + 4 * listed), rows * listed * heads
        ),
        name="last_own" if own else "last_other",
    )(core, query, *pieces, *state)


def join_kernel(core_ref, got_ref, _, out_ref):
    out_ref[...] = got_ref[...]


def join_columns(core, got, partial):
    rows, half = got.shape
    step = 128
    return pl.pallas_call(
        join_kernel,
        out_shape=jax.ShapeDtypeStruct(partial.shape, partial.dtype),
        grid_spec=pltpu.PrefetchScalarGridSpec(
            num_scalar_prefetch=1,
            grid=(rows // step,),
            in_specs=[
                pl.BlockSpec((step, half), lambda i, c: (i, 0)),
                pl.BlockSpec(memory_space=pl.ANY),
            ],
            out_specs=pl.BlockSpec((step, half), lambda i, c: (i, 1 - c[0])),
        ),
        input_output_aliases={2: 0},
        cost_estimate=cost(0, 4 * rows * half, 0),
        name="join_columns",
    )(core, got, partial)


def on_device(queries, keys_values, offsets, ref_owner, ref_slot):
    rows, columns = queries.shape
    half = columns // 2
    blocks = rows // BLK
    margin = REACH * BLK
    frames = lax.axis_size("frame")
    me = lax.axis_index("frame")
    core = me % 2
    partner = me + 1 - 2 * core
    chips = frames // 2
    chip = me // 2
    core_arg = core.reshape(1).astype(jnp.int32)
    swap = [(i, i ^ 1) for i in range(frames)]

    mine, theirs = split_columns(core_arg, keys_values)
    other = lax.ppermute(theirs, "frame", swap)
    q_other = lax.ppermute(
        lax.dynamic_slice_in_dim(queries, (1 - core) * half, half, 1), "frame", swap
    )
    offsets_other = lax.ppermute(offsets, "frame", swap)

    order = list(range(0, chips, 2)) + list(range(chips - 1 - chips % 2, 0, -2))
    place = jnp.where(chip % 2 == 0, chip // 2, chips - 1 - chip // 2)
    owner_chip = ref_owner // 2
    owner_place = jnp.where(owner_chip % 2 == 0, owner_chip // 2, chips - 1 - owner_chip // 2)

    def ring(step):
        return [
            (2 * order[i] + c, 2 * order[(i + step) % chips] + c)
            for c in range(2)
            for i in range(chips)
        ]

    up, down = ring(1), ring(-1)
    reach = chips // 2
    piece_rows = NREF * REFLEN // chips
    per_ref = REFLEN // piece_rows
    cut = piece_rows // 2

    def held(piece, low, size):
        piece = piece % chips
        ref = piece // per_ref
        start = ref_slot[ref] * BLK + (piece % per_ref) * piece_rows + low
        own = lax.dynamic_slice_in_dim(mine, start, size, 1)
        near = lax.dynamic_slice_in_dim(other, start, size, 1)
        return ref_owner[ref] == me, ref_owner[ref] == partner, own, near

    def offer(piece, low, size):
        _, is_near, own, near = held(piece, low, size)
        return jnp.where(is_near, near, own)

    def merge(piece, low, size, got):
        is_own, is_near, own, near = held(piece, low, size)
        return jnp.where(is_own, own, jnp.where(is_near, near, got))

    send_up = offer(place + reach, 0, cut)
    send_down = offer(place + reach, cut, cut)
    for step in range(reach):
        if step == 1:
            piece = place + reach - 1
            send_up = jnp.concatenate(
                [merge(piece, 0, cut, got_up), offer(piece, cut, cut)], 1
            )
            piece = place + reach + 1
            send_down = jnp.concatenate(
                [offer(piece, 0, cut), merge(piece, cut, cut, got_down)], 1
            )
        elif step > 1:
            send_up = merge(place + reach - step, 0, piece_rows, got_up)
            send_down = merge(place + reach + step, 0, piece_rows, got_down)
        got_up = lax.ppermute(send_up, "frame", up)
        got_down = lax.ppermute(send_down, "frame", down)
    away = (place - owner_place[place // per_ref]) % chips
    row = lax.broadcasted_iota(jnp.int32, (1, piece_rows, 1), 1)
    from_below = (away < reach) | ((away == reach) & (row < cut))
    own_piece = merge(place, 0, piece_rows, jnp.where(from_below, got_up, got_down))

    along = [(2 * i + c, 2 * i + 2 + c) for i in range(chips - 1) for c in range(2)]
    back = [(b, a) for a, b in along]
    tail = jnp.where(core == 1, mine[:, rows - margin :], other[:, rows - margin :])
    head = jnp.where(core == 0, mine[:, :margin], other[:, :margin])
    left = lax.ppermute(tail, "frame", along)
    right = lax.ppermute(head, "frame", back)

    first = jnp.stack([me, partner]) * blocks
    listed = jnp.concatenate(
        [jnp.zeros((2, blocks, 1), jnp.int32), jnp.stack([offsets, offsets_other])], 2
    )
    target = (first[:, None] + jnp.arange(blocks, dtype=jnp.int32))[:, :, None] + listed
    usable = (target >= 0) & (target < frames * blocks)
    table = jnp.concatenate(
        [
            core_arg,
            (target - chip * 2 * blocks + REACH).reshape(-1).astype(jnp.int32),
            usable.reshape(-1).astype(jnp.int32),
        ]
    )
    state = window_part(table, queries, q_other, mine, other, left, right)

    send_up = send_down = own_piece
    fresh = [own_piece]
    for step in range(reach):
        if step == reach - 1:
            send_up, send_down = send_up[:, :cut], send_down[:, cut:]
        send_up = lax.ppermute(send_up, "frame", up)
        send_down = lax.ppermute(send_down, "frame", down)
        fresh = fresh + [send_up, send_down]
        if step < reach - 1:
            state = ref_part(core_arg, queries, q_other, fresh, state)
            fresh = []

    out_other = last_part(core_arg, q_other, False, fresh, state)
    got = lax.ppermute(out_other, "frame", swap)
    out = last_part(core_arg, queries, True, fresh, state)
    return join_columns(core_arg, got, out)


def solution(mesh):
    placed = (
        P(("groups", "frame"), None),
        P(("groups", "frame"), None, None),
        P(("groups", "frame"), None),
        P("groups"),
        P("groups"),
    )
    return jax.shard_map(
        on_device,
        mesh=mesh,
        in_specs=placed,
        out_specs=P(("groups", "frame"), None),
        check_vma=False,
    )
```
